32 devices in a mesh: perm: 2 (over y), subj: 8 (over z, core), vert: 2 (over x).
Axes of the slice: x: 2, y: 2, z: 4, core: 2. Of those that a mesh axis runs over, the one named last changes fastest.
Arguments:
- kinship: bfloat16 [2048, 2048], P('subj')
- phenotype: bfloat16 [2048, 2048], P('subj', 'vert')
- shuffle: int32 [4096], P(('perm', 'subj')), parts along dimension 0, may hold values from 0 to 2047, as said below
Outputs:
- statistic: float32 [4096], P(('perm', 'vert')), parts along dimension 0
The draws below stay inside these ranges and needn't reach their ends.
There are 2 independent parts, one for each index of `perm`. The reference program is written for one: setup_inputs(seed, part) draws one part's arguments, and reference() takes and returns one part's arrays. A program takes and returns all parts, laid end to end along the dimension named above; an argument that names none is the same for every part. Nothing has to cross between parts.
Inputs may be any that keep to these rules, and one draw needn't show every extreme that they name: shuffle is a permutation of 0 to 2047 that maps every subject into its own exchangeability block.
All inputs are finite; a program needn't handle non-finite values.
Results may differ from the reference program's by a relative error of at most 0.0003.
Values may be sent and summed in bfloat16 or wider, within the bound.
A program may use at most 128 MiB of HBM per device.

```python
import jax
import jax.numpy as jnp
from jax import lax

BLOCKS = 16
SUBJECTS = 2048
VERTICES = 2048


def draw_kinship(key, part):
    key_noise, key_diag = jax.random.split(key)
    entries = jax.random.normal(key_noise, (SUBJECTS, SUBJECTS), jnp.float32)
    symmetric = 0.4 * (entries + entries.T) / jnp.sqrt(2.0 * SUBJECTS)
    diagonal = 0.8 + 0.4 * jax.random.uniform(key_diag, (SUBJECTS,), jnp.float32)
    identity = jnp.eye(SUBJECTS, dtype=jnp.float32)
    return (symmetric * (1.0 - identity) + identity * diagonal[:, None]).astype(jnp.bfloat16)


def draw_phenotype(key, part):
    key_noise, key_rows, key_cols = jax.random.split(key, 3)
    entries = jax.random.normal(key_noise, (SUBJECTS, VERTICES), jnp.float32)
    position = jnp.arange(SUBJECTS, dtype=jnp.float32) / SUBJECTS
    row_scale = jnp.exp(1.0986123 * position + 2.3025851 * jax.random.uniform(key_rows, (SUBJECTS,), jnp.float32)) / 4.0
    col_scale = jnp.exp(2.3025851 * jax.random.uniform(key_cols, (VERTICES,), jnp.float32)) / 3.0
    return (entries * row_scale[:, None] * col_scale[None, :]).astype(jnp.bfloat16)


def draw_shuffle(key, part):
    key_block, key_rank = jax.random.split(key)
    block_ids = jax.random.randint(key_block, (SUBJECTS,), 0, BLOCKS).astype(jnp.int32)
    ranks = jax.random.permutation(key_rank, SUBJECTS).astype(jnp.int32)
    positions = jnp.arange(SUBJECTS, dtype=jnp.int32)
    source_order = jnp.argsort(block_ids * SUBJECTS + ranks, stable=True).astype(jnp.int32)
    target_order = jnp.argsort(block_ids * SUBJECTS + positions, stable=True).astype(jnp.int32)
    return jnp.zeros((SUBJECTS,), jnp.int32).at[target_order].set(source_order)


def setup_inputs(seed: int = 0, part: int = 0) -> dict:
    streams_of = jax.random.split(jax.random.key(seed), 4)
    part_splits = jax.random.split(jax.random.fold_in(streams_of[3], part), 4)
    kinship = draw_kinship(jax.random.fold_in(streams_of[3], 71), part)
    phenotype = draw_phenotype(jax.random.fold_in(streams_of[3], 71), part)
    shuffle = draw_shuffle(jax.random.fold_in(jax.random.fold_in(streams_of[3], part), 71), part)
    return dict(kinship=kinship, phenotype=phenotype, shuffle=shuffle)


def reference(kinship, phenotype, shuffle):
    permuted = jnp.take(phenotype, shuffle.astype(jnp.int32), axis=0)
    product = jnp.dot(kinship, permuted, preferred_element_type=jnp.float32)
    kin_diag = jnp.diagonal(kinship).astype(jnp.float32)
    moved = permuted.astype(jnp.float32)
    cross_term = lax.optimization_barrier(jnp.sum(moved * (product - kin_diag[:, None] * moved), axis=0))
    values = phenotype.astype(jnp.float32)
    squares = lax.optimization_barrier(jnp.sum(values * values, axis=0))
    subject_count = kinship.shape[0]
    return cross_term / (jnp.sqrt(jnp.float32(subject_count)) * (squares / subject_count + 1e-05))
```

```python
import functools

import jax
import jax.numpy as jnp
from jax import lax
from jax.experimental import pallas as pl
from jax.experimental.pallas import tpu as pltpu
from jax.sharding import PartitionSpec as P

MESH = pl.DeviceIdType.MESH
CORES = 2
HALVES = 2


def kernel(
    n_perm, n_subj,
    kin_ref, phe_ref, shf_ref, out_ref,
    shuf, scol, moved_kin, gathered, acc, parts, final,
    shuf_send, shuf_recv, own_send, row_send, sib_send, row_recv, fin_send, fin_recv,
):
    perm, subj = lax.axis_index("perm"), lax.axis_index("subj")
    n_all = n_perm * n_subj
    me = perm * n_subj + subj
    z, core = subj // CORES, subj % CORES
    n_z = n_subj // CORES
    sibling = z * CORES + (1 - core)
    rows = kin_ref.shape[0]
    cols = gathered.shape[2]
    piece = rows // HALVES
    first_col = pl.multiple_of(perm * cols, cols)
    n_events = HALVES * (n_z - 1)

    def partner(k):
        other = lax.rem(me + k, n_all)
        return other, {"perm": other // n_subj, "subj": lax.rem(other, n_subj)}

    barrier = pltpu.get_barrier_semaphore()

    @pl.loop(1, n_all)
    def _(k):
        pl.semaphore_signal(barrier, inc=1, device_id=partner(k)[1], device_id_type=MESH)

    pl.semaphore_wait(barrier, n_all - 1)

    def half(h):
        return pl.ds(pl.multiple_of(h * piece, piece), piece)

    def own_copy(h, way, target):
        return pltpu.make_async_remote_copy(
            src_ref=phe_ref.at[half(h), pl.ds(first_col, cols)],
            dst_ref=gathered.at[subj, half(h)],
            send_sem=own_send.at[way, h], recv_sem=row_recv.at[subj, h],
            device_id={"subj": target}, device_id_type=MESH)

    def pass_copy(slot, h, sems, target):
        return pltpu.make_async_remote_copy(
            src_ref=gathered.at[slot, half(h)], dst_ref=gathered.at[slot, half(h)],
            send_sem=sems.at[slot, h], recv_sem=row_recv.at[slot, h],
            device_id={"subj": target}, device_id_type=MESH)

    def shuf_copy(k, slot):
        return pltpu.make_async_remote_copy(
            src_ref=shf_ref, dst_ref=shuf.at[slot],
            send_sem=shuf_send.at[k], recv_sem=shuf_recv.at[slot],
            device_id=partner(k)[1], device_id_type=MESH)

    @pl.loop(1, n_all)
    def _(k):
        shuf_copy(k, me).start()

    def own_sends(act):
        for h in range(HALVES):
            @pl.when(z > 0)
            def _():
                act(own_copy(h, 0, subj - CORES))

            @pl.when(z < n_z - 1)
            def _():
                act(own_copy(h, 1, subj + CORES))

            act(own_copy(h, 2, sibling))

    own_sends(lambda copy: copy.start())
    shuf[me] = shf_ref[...]
    own = phe_ref[:, pl.ds(first_col, cols)]
    gathered[subj] = own
    own32 = own.astype(jnp.float32)
    squares = jnp.sum(own32 * own32, axis=0, keepdims=True)
    for p in range(n_perm):
        parts[p, 1:2] = squares
    own_cols = pl.ds(pl.multiple_of(subj * rows, rows), rows)
    down = lax.broadcasted_iota(jnp.int32, (rows, rows), 0)
    across = lax.broadcasted_iota(jnp.int32, (rows, rows), 1)
    kin_diag = jnp.sum(
        jnp.where(down == across, kin_ref[:, own_cols].astype(jnp.float32), 0.0),
        axis=1, keepdims=True)

    @pl.loop(1, n_all)
    def _(k):
        shuf_copy(k, partner(k)[0]).wait_recv()

    for p in range(n_perm):
        mine = shuf[p * n_subj + subj]
        scol[p] = jnp.transpose(jnp.broadcast_to(mine, (rows, rows)))

    def move(task):
        p, block = task // n_subj, lax.rem(task, n_subj)
        base = down + block * rows
        picks = jnp.concatenate(
            [(base == shuf[p * n_subj + j]).astype(jnp.bfloat16) for j in range(n_subj)],
            axis=1)
        kin = lax.dot_general(
            kin_ref[...], picks, (((1,), (1,)), ((), ())),
            preferred_element_type=jnp.float32)
        at = pl.multiple_of(p * 2 * rows, 2 * rows)
        moved_kin[block, pl.ds(at, rows)] = kin.astype(jnp.bfloat16)
        picker = (scol[p] == across + block * rows).astype(jnp.bfloat16)
        moved_kin[block, pl.ds(at + rows, rows)] = picker

    def event(e, act):
        dist, h = e // HALVES + 1, lax.rem(e, HALVES)

        @pl.when(z + dist < n_z)
        def _():
            act(subj + CORES * dist, h, z > 0, subj - CORES)

        @pl.when(z - dist >= 0)
        def _():
            act(subj - CORES * dist, h, z < n_z - 1, subj + CORES)

    def arrive(slot, h, onward, target):
        pass_copy(slot, h, row_send, sibling).wait_recv()

        @pl.when(onward)
        def _():
            pass_copy(slot, h, row_send, target).start()

        pass_copy(slot, h, sib_send, sibling).start()

    def drain(slot, h, onward, target):
        @pl.when(onward)
        def _():
            pass_copy(slot, h, row_send, target).wait_send()

        pass_copy(slot, h, sib_send, sibling).wait_send()

    def add(slot):
        acc[...] += jnp.dot(
            moved_kin[slot], gathered[slot], preferred_element_type=jnp.float32)

    def await_sibling(slot):
        for h in range(HALVES):
            pass_copy(slot, h, row_send, sibling).wait_recv()

    def add_dist(dist):
        def pair(slot, other):
            add(slot)
            await_sibling(other)
            add(other)

        flip = sibling - subj

        @pl.when(z + dist < n_z)
        def _():
            pair(subj + CORES * dist, subj + CORES * dist + flip)

        @pl.when(jnp.logical_and(z - dist >= 0, dist > 0))
        def _():
            pair(subj - CORES * dist, subj - CORES * dist + flip)

    n_tasks = n_perm * n_subj
    per_event = n_tasks // n_z
    acc[...] = jnp.zeros_like(acc)

    @pl.loop(0, n_z)
    def _(e):
        @pl.loop(0, per_event)
        def _(t):
            move(e * per_event + t)

        event(e, arrive)

    @pl.loop(n_z, n_events)
    def _(e):
        add_dist(e - n_z)
        event(e, arrive)

    @pl.loop(n_events - n_z, n_z)
    def _(dist):
        add_dist(dist)

    for p in range(n_perm):
        at = p * 2 * rows
        moved = acc[at + rows:at + 2 * rows]
        cross = jnp.sum(moved * (acc[at:at + rows] - kin_diag * moved), axis=0, keepdims=True)
        parts[p, 0:1] = cross

    def fin_copy(k, slot):
        other, device = partner(k)
        return pltpu.make_async_remote_copy(
            src_ref=parts.at[other // n_subj], dst_ref=final.at[slot],
            send_sem=fin_send.at[k], recv_sem=fin_recv.at[slot],
            device_id=device, device_id_type=MESH)

    @pl.loop(1, n_all)
    def _(k):
        fin_copy(k, me).start()

    final[me] = parts[perm]
    own_sends(lambda copy: copy.wait_send())

    @pl.loop(0, n_events)
    def _(e):
        event(e, drain)

    @pl.loop(1, n_all)
    def _(k):
        shuf_copy(k, me).wait_send()

    @pl.loop(1, n_all)
    def _(k):
        fin_copy(k, partner(k)[0]).wait_recv()

    count = n_subj * rows
    for q in range(n_perm):
        total = jnp.sum(final[q * n_subj:(q + 1) * n_subj], axis=0)
        scale = jnp.sqrt(jnp.float32(count)) * (total[1:2] / count + 1e-05)
        out_ref[:, q * cols:(q + 1) * cols] = total[0:1] / scale

    @pl.loop(1, n_all)
    def _(k):
        fin_copy(k, me).wait_send()


def per_device(n_perm, n_subj, kinship, phenotype, shuffle):
    rows, width = phenotype.shape
    cols = width // n_perm
    n_all = n_perm * n_subj
    DMA = pltpu.SemaphoreType.DMA
    out = pl.pallas_call(
        functools.partial(kernel, n_perm, n_subj),
        out_shape=jax.ShapeDtypeStruct((1, width), jnp.float32),
        in_specs=[pl.BlockSpec(memory_space=pltpu.VMEM)] * 3,
        out_specs=pl.BlockSpec(memory_space=pltpu.VMEM),
        scratch_shapes=[
            pltpu.VMEM((n_all, 1, rows), jnp.int32),
            pltpu.VMEM((n_perm, rows, rows), jnp.int32),
            pltpu.VMEM((n_subj, n_perm * 2 * rows, rows), jnp.bfloat16),
            pltpu.VMEM((n_subj, rows, cols), jnp.bfloat16),
            pltpu.VMEM((n_perm * 2 * rows, cols), jnp.float32),
            pltpu.VMEM((n_perm, 2, cols), jnp.float32),
            pltpu.VMEM((n_all, 2, cols), jnp.float32),
            DMA((n_all,)), DMA((n_all,)),
            DMA((3, HALVES)),
            DMA((n_subj, HALVES)), DMA((n_subj, HALVES)), DMA((n_subj, HALVES)),
            DMA((n_all,)), DMA((n_all,)),
        ],
        compiler_params=pltpu.CompilerParams(collective_id=0, has_side_effects=True),
    )(kinship, phenotype, shuffle.reshape(1, rows))
    return out.reshape(width)


def solution(mesh):
    in_specs = (P("subj", None), P("subj", "vert"), P(("perm", "subj")))
    out_specs = P(("perm", "vert"))
    body = functools.partial(per_device, mesh.shape["perm"], mesh.shape["subj"])
    return jax.shard_map(body, mesh=mesh, in_specs=in_specs, out_specs=out_specs, check_vma=False)
```

```python
import functools

import jax
import jax.numpy as jnp
from jax import lax
from jax.experimental import pallas as pl
from jax.experimental.pallas import tpu as pltpu
from jax.sharding import PartitionSpec as P

MESH = pl.DeviceIdType.MESH
CORES = 2
HALVES = 4


def kernel(
    n_perm, n_subj,
    kin_hbm, phe_ref, shf_ref, out_ref,
    kin_ref, load_sem, shuf, scol, moved_kin, gathered, acc, parts, final,
    shuf_send, shuf_recv, own_send, row_send, sib_send, row_recv, fin_send, fin_recv,
):
    perm, subj = lax.axis_index("perm"), lax.axis_index("subj")
    n_all = n_perm * n_subj
    me = perm * n_subj + subj
    z, core = subj // CORES, subj % CORES
    n_z = n_subj // CORES
    sibling = z * CORES + (1 - core)
    rows = kin_ref.shape[0]
    cols = gathered.shape[2]
    piece = rows // HALVES
    first_col = pl.multiple_of(perm * cols, cols)
    n_events = HALVES * (n_z - 1)

    def partner(k):
        other = lax.rem(me + k, n_all)
        return other, {"perm": other // n_subj, "subj": lax.rem(other, n_subj)}

    loads = (
        pltpu.make_async_copy(
            phe_ref.at[:, pl.ds(first_col, cols)], gathered.at[subj], load_sem.at[0]),
        pltpu.make_async_copy(kin_hbm, kin_ref, load_sem.at[1]),
    )
    for load in loads:
        load.start()
    barrier = pltpu.get_barrier_semaphore()

    @pl.loop(1, n_all)
    def _(k):
        pl.semaphore_signal(barrier, inc=1, device_id=partner(k)[1], device_id_type=MESH)

    pl.semaphore_wait(barrier, n_all - 1)

    def half(h):
        return pl.ds(pl.multiple_of(h * piece, piece), piece)

    def own_copy(h, way, target):
        return pltpu.make_async_remote_copy(
            src_ref=phe_ref.at[half(h), pl.ds(first_col, cols)],
            dst_ref=gathered.at[subj, half(h)],
            send_sem=own_send.at[way, h], recv_sem=row_recv.at[subj, h],
            device_id={"subj": target}, device_id_type=MESH)

    def pass_copy(slot, h, sems, target):
        return pltpu.make_async_remote_copy(
            src_ref=gathered.at[slot, half(h)], dst_ref=gathered.at[slot, half(h)],
            send_sem=sems.at[slot, h], recv_sem=row_recv.at[slot, h],
            device_id={"subj": target}, device_id_type=MESH)

    def shuf_copy(k, slot):
        return pltpu.make_async_remote_copy(
            src_ref=shf_ref, dst_ref=shuf.at[slot],
            send_sem=shuf_send.at[k], recv_sem=shuf_recv.at[slot],
            device_id=partner(k)[1], device_id_type=MESH)

    @pl.loop(1, n_all)
    def _(k):
        shuf_copy(k, me).start()

    def own_sends(act):
        for h in range(HALVES):
            @pl.when(z > 0)
            def _():
                act(own_copy(h, 0, subj - CORES))

            @pl.when(z < n_z - 1)
            def _():
                act(own_copy(h, 1, subj + CORES))

            act(own_copy(h, 2, sibling))

    own_sends(lambda copy: copy.start())
    shuf[me] = shf_ref[...]
    for load in loads:
        load.wait()
    own32 = gathered[subj].astype(jnp.float32)
    squares = jnp.sum(own32 * own32, axis=0, keepdims=True)
    for p in range(n_perm):
        parts[p, 1:2] = squares
    own_cols = pl.ds(pl.multiple_of(subj * rows, rows), rows)
    down = lax.broadcasted_iota(jnp.int32, (rows, rows), 0)
    across = lax.broadcasted_iota(jnp.int32, (rows, rows), 1)
    kin_diag = jnp.sum(
        jnp.where(down == across, kin_ref[:, own_cols].astype(jnp.float32), 0.0),
        axis=1, keepdims=True)

    @pl.loop(1, n_all)
    def _(k):
        shuf_copy(k, partner(k)[0]).wait_recv()

    for p in range(n_perm):
        mine = shuf[p * n_subj + subj]
        scol[p] = jnp.transpose(jnp.broadcast_to(mine, (rows, rows)))

    def move(task):
        p, block = task // n_subj, lax.rem(task, n_subj)
        base = down + block * rows
        picks = jnp.concatenate(
            [(base == shuf[p * n_subj + j]).astype(jnp.bfloat16) for j in range(n_subj)],
            axis=1)
        kin = lax.dot_general(
            kin_ref[...], picks, (((1,), (1,)), ((), ())),
            preferred_element_type=jnp.float32)
        at = pl.multiple_of(p * 2 * rows, 2 * rows)
        moved_kin[block, pl.ds(at, rows)] = kin.astype(jnp.bfloat16)
        picker = (scol[p] == across + block * rows).astype(jnp.bfloat16)
        moved_kin[block, pl.ds(at + rows, rows)] = picker

    def event(e, act):
        dist, h = e // HALVES + 1, lax.rem(e, HALVES)

        @pl.when(z + dist < n_z)
        def _():
            act(subj + CORES * dist, h, z > 0, subj - CORES)

        @pl.when(z - dist >= 0)
        def _():
            act(subj - CORES * dist, h, z < n_z - 1, subj + CORES)

    def arrive(slot, h, onward, target):
        pass_copy(slot, h, row_send, sibling).wait_recv()

        @pl.when(onward)
        def _():
            pass_copy(slot, h, row_send, target).start()

        pass_copy(slot, h, sib_send, sibling).start()

    def drain(slot, h, onward, target):
        @pl.when(onward)
        def _():
            pass_copy(slot, h, row_send, target).wait_send()

        pass_copy(slot, h, sib_send, sibling).wait_send()

    def add(slot):
        acc[...] += jnp.dot(
            moved_kin[slot], gathered[slot], preferred_element_type=jnp.float32)

    def await_sibling(slot):
        for h in range(HALVES):
            pass_copy(slot, h, row_send, sibling).wait_recv()

    def add_dist(dist):
        def pair(slot, other):
            add(slot)
            await_sibling(other)
            add(other)

        flip = sibling - subj

        @pl.when(z + dist < n_z)
        def _():
            pair(subj + CORES * dist, subj + CORES * dist + flip)

        @pl.when(jnp.logical_and(z - dist >= 0, dist > 0))
        def _():
            pair(subj - CORES * dist, subj - CORES * dist + flip)

    n_tasks = n_perm * n_subj
    early = HALVES * n_z // 2
    per_event = n_tasks // early
    n_mixed = min(n_z - 1, n_events - early, early // (HALVES - 1) + 1)
    acc[...] = jnp.zeros_like(acc)

    @pl.loop(0, early)
    def _(e):
        @pl.loop(0, per_event)
        def _(t):
            move(e * per_event + t)

        event(e, arrive)

    @pl.loop(early, early + n_mixed)
    def _(e):
        add_dist(e - early)
        event(e, arrive)

    @pl.loop(early + n_mixed, n_events)
    def _(e):
        event(e, arrive)

    @pl.loop(n_mixed, n_z)
    def _(dist):
        add_dist(dist)

    for p in range(n_perm):
        at = p * 2 * rows
        moved = acc[at + rows:at + 2 * rows]
        cross = jnp.sum(moved * (acc[at:at + rows] - kin_diag * moved), axis=0, keepdims=True)
        parts[p, 0:1] = cross

    def fin_copy(k, slot):
        other, device = partner(k)
        return pltpu.make_async_remote_copy(
            src_ref=parts.at[other // n_subj], dst_ref=final.at[slot],
            send_sem=fin_send.at[k], recv_sem=fin_recv.at[slot],
            device_id=device, device_id_type=MESH)

    @pl.loop(1, n_all)
    def _(k):
        fin_copy(k, me).start()

    final[me] = parts[perm]
    own_sends(lambda copy: copy.wait_send())

    @pl.loop(0, n_events)
    def _(e):
        event(e, drain)

    @pl.loop(1, n_all)
    def _(k):
        shuf_copy(k, me).wait_send()

    @pl.loop(1, n_all)
    def _(k):
        fin_copy(k, partner(k)[0]).wait_recv()

    count = n_subj * rows
    for q in range(n_perm):
        total = jnp.sum(final[q * n_subj:(q + 1) * n_subj], axis=0)
        scale = jnp.sqrt(jnp.float32(count)) * (total[1:2] / count + 1e-05)
        out_ref[:, q * cols:(q + 1) * cols] = total[0:1] / scale

    @pl.loop(1, n_all)
    def _(k):
        fin_copy(k, me).wait_send()


def per_device(n_perm, n_subj, kinship, phenotype, shuffle):
    rows, width = phenotype.shape
    cols = width // n_perm
    n_all = n_perm * n_subj
    DMA = pltpu.SemaphoreType.DMA
    out = pl.pallas_call(
        functools.partial(kernel, n_perm, n_subj),
        out_shape=jax.ShapeDtypeStruct((1, width), jnp.float32),
        in_specs=[pl.BlockSpec(memory_space=pl.ANY)] * 2 + [pl.BlockSpec(memory_space=pltpu.VMEM)],
        out_specs=pl.BlockSpec(memory_space=pltpu.VMEM),
        scratch_shapes=[
            pltpu.VMEM(kinship.shape, jnp.bfloat16),
            DMA((2,)),
            pltpu.VMEM((n_all, 1, rows), jnp.int32),
            pltpu.VMEM((n_perm, rows, rows), jnp.int32),
            pltpu.VMEM((n_subj, n_perm * 2 * rows, rows), jnp.bfloat16),
            pltpu.VMEM((n_subj, rows, cols), jnp.bfloat16),
            pltpu.VMEM((n_perm * 2 * rows, cols), jnp.float32),
            pltpu.VMEM((n_perm, 2, cols), jnp.float32),
            pltpu.VMEM((n_all, 2, cols), jnp.float32),
            DMA((n_all,)), DMA((n_all,)),
            DMA((3, HALVES)),
            DMA((n_subj, HALVES)), DMA((n_subj, HALVES)), DMA((n_subj, HALVES)),
            DMA((n_all,)), DMA((n_all,)),
        ],
        compiler_params=pltpu.CompilerParams(collective_id=0, has_side_effects=True),
    )(kinship, phenotype, shuffle.reshape(1, rows))
    return out.reshape(width)


def solution(mesh):
    in_specs = (P("subj", None), P("subj", "vert"), P(("perm", "subj")))
    out_specs = P(("perm", "vert"))
    body = functools.partial(per_device, mesh.shape["perm"], mesh.shape["subj"])
    return jax.shard_map(body, mesh=mesh, in_specs=in_specs, out_specs=out_specs, check_vma=False)
```

```python
import functools

import jax
import jax.numpy as jnp
from jax import lax
from jax.experimental import pallas as pl
from jax.experimental.pallas import tpu as pltpu
from jax.sharding import PartitionSpec as P

MESH = pl.DeviceIdType.MESH
CORES = 2
HALVES = 4
BEFORE = 2


def kernel(
    n_perm, n_subj,
    kin_hbm, phe_ref, shf_ref, out_ref,
    kin_ref, load_sem, waves, shuf, scol, moved_kin, gathered, acc, parts, final,
    shuf_send, shuf_recv, own_send, row_send, sib_send, row_recv, fin_send, fin_recv,
):
    perm, subj = lax.axis_index("perm"), lax.axis_index("subj")
    n_all = n_perm * n_subj
    me = perm * n_subj + subj
    z, core = subj // CORES, subj % CORES
    n_z = n_subj // CORES
    sibling = z * CORES + (1 - core)
    rows = kin_ref.shape[0]
    cols = gathered.shape[2]
    piece = rows // HALVES
    first_col = pl.multiple_of(perm * cols, cols)
    n_events = HALVES * (n_z - 1)

    def partner(k):
        other = lax.rem(me + k, n_all)
        return other, {"perm": other // n_subj, "subj": lax.rem(other, n_subj)}

    loads = (
        pltpu.make_async_copy(
            phe_ref.at[:, pl.ds(first_col, cols)], gathered.at[subj], load_sem.at[0]),
        pltpu.make_async_copy(kin_hbm, kin_ref, load_sem.at[1]),
    )
    for load in loads:
        load.start()
    barrier = pltpu.get_barrier_semaphore()

    has_left, has_right = z > 0, z < n_z - 1

    def signal(sem, **device):
        pl.semaphore_signal(sem, inc=1, device_id=device, device_id_type=MESH)

    def signal_perms(sem):
        for k in range(1, n_perm):
            signal(sem, perm=lax.rem(perm + k, n_perm))

    @pl.when(has_left)
    def _():
        signal(barrier, subj=subj - CORES)

    @pl.when(has_right)
    def _():
        signal(barrier, subj=subj + CORES)

    signal(barrier, subj=sibling)
    signal_perms(barrier)
    pl.semaphore_wait(
        barrier, n_perm + has_left.astype(jnp.int32) + has_right.astype(jnp.int32))

    def wave_right():
        @pl.when(has_left)
        def _():
            pl.semaphore_wait(waves.at[0], 1)

        @pl.when(has_right)
        def _():
            signal(waves.at[0], subj=subj + CORES)

    def wave_left():
        @pl.when(has_right)
        def _():
            pl.semaphore_wait(waves.at[1], 1)

        @pl.when(has_left)
        def _():
            signal(waves.at[1], subj=subj - CORES)

    def all_ready():
        @pl.when(z < n_z // 2)
        def _():
            wave_right()
            wave_left()

        @pl.when(z >= n_z // 2)
        def _():
            wave_left()
            wave_right()

        signal(waves.at[2], subj=sibling)
        pl.semaphore_wait(waves.at[2], 1)
        signal_perms(waves.at[3])
        pl.semaphore_wait(waves.at[3], n_perm - 1)

    def half(h):
        return pl.ds(pl.multiple_of(h * piece, piece), piece)

    def own_copy(h, way, target):
        return pltpu.make_async_remote_copy(
            src_ref=phe_ref.at[half(h), pl.ds(first_col, cols)],
            dst_ref=gathered.at[subj, half(h)],
            send_sem=own_send.at[way, h], recv_sem=row_recv.at[subj, h],
            device_id={"subj": target}, device_id_type=MESH)

    def pass_copy(slot, h, sems, target):
        return pltpu.make_async_remote_copy(
            src_ref=gathered.at[slot, half(h)], dst_ref=gathered.at[slot, half(h)],
            send_sem=sems.at[slot, h], recv_sem=row_recv.at[slot, h],
            device_id={"subj": target}, device_id_type=MESH)

    def shuf_copy(k, slot):
        return pltpu.make_async_remote_copy(
            src_ref=shf_ref, dst_ref=shuf.at[slot],
            send_sem=shuf_send.at[k], recv_sem=shuf_recv.at[slot],
            device_id=partner(k)[1], device_id_type=MESH)

    def own_sends(first, last, act):
        for h in range(first, last):
            @pl.when(z > 0)
            def _():
                act(own_copy(h, 0, subj - CORES))

            @pl.when(z < n_z - 1)
            def _():
                act(own_copy(h, 1, subj + CORES))

            act(own_copy(h, 2, sibling))

    own_sends(0, HALVES - 1, lambda copy: copy.start())
    all_ready()

    @pl.loop(1, n_all)
    def _(k):
        shuf_copy(k, me).start()

    own_sends(HALVES - 1, HALVES, lambda copy: copy.start())
    shuf[me] = shf_ref[...]
    for load in loads:
        load.wait()
    own32 = gathered[subj].astype(jnp.float32)
    squares = jnp.sum(own32 * own32, axis=0, keepdims=True)
    for p in range(n_perm):
        parts[p, 1:2] = squares
    own_cols = pl.ds(pl.multiple_of(subj * rows, rows), rows)
    down = lax.broadcasted_iota(jnp.int32, (rows, rows), 0)
    across = lax.broadcasted_iota(jnp.int32, (rows, rows), 1)
    kin_diag = jnp.sum(
        jnp.where(down == across, kin_ref[:, own_cols].astype(jnp.float32), 0.0),
        axis=1, keepdims=True)

    def move(task):
        p, block = task // n_subj, lax.rem(task, n_subj)
        base = down + block * rows
        picks = jnp.concatenate(
            [(base == shuf[p * n_subj + j]).astype(jnp.bfloat16) for j in range(n_subj)],
            axis=1)
        kin = lax.dot_general(
            kin_ref[...], picks, (((1,), (1,)), ((), ())),
            preferred_element_type=jnp.float32)
        at = pl.multiple_of(p * 2 * rows, 2 * rows)
        moved_kin[block, pl.ds(at, rows)] = kin.astype(jnp.bfloat16)
        picker = (scol[p] == across + block * rows).astype(jnp.bfloat16)
        moved_kin[block, pl.ds(at + rows, rows)] = picker

    def event(e, act):
        dist, h = e // HALVES + 1, lax.rem(e, HALVES)

        @pl.when(z + dist < n_z)
        def _():
            act(subj + CORES * dist, h, z > 0, subj - CORES)

        @pl.when(z - dist >= 0)
        def _():
            act(subj - CORES * dist, h, z < n_z - 1, subj + CORES)

    def arrive(slot, h, onward, target):
        pass_copy(slot, h, row_send, sibling).wait_recv()

        @pl.when(onward)
        def _():
            pass_copy(slot, h, row_send, target).start()

        pass_copy(slot, h, sib_send, sibling).start()

    def drain(slot, h, onward, target):
        @pl.when(onward)
        def _():
            pass_copy(slot, h, row_send, target).wait_send()

        pass_copy(slot, h, sib_send, sibling).wait_send()

    def add(slot):
        acc[...] += jnp.dot(
            moved_kin[slot], gathered[slot], preferred_element_type=jnp.float32)

    def await_sibling(slot):
        for h in range(HALVES):
            pass_copy(slot, h, row_send, sibling).wait_recv()

    def add_dist(dist):
        def pair(slot, other):
            add(slot)
            await_sibling(other)
            add(other)

        flip = sibling - subj

        @pl.when(z + dist < n_z)
        def _():
            pair(subj + CORES * dist, subj + CORES * dist + flip)

        @pl.when(jnp.logical_and(z - dist >= 0, dist > 0))
        def _():
            pair(subj - CORES * dist, subj - CORES * dist + flip)

    n_tasks = n_perm * n_subj
    busy = HALVES * n_z // 2
    per_event = n_tasks // busy
    early = min(BEFORE + busy, n_events)
    n_mixed = min(n_z - 1, n_events - early, early // (HALVES - 1) + 1)
    acc[...] = jnp.zeros_like(acc)
    for e in range(BEFORE):
        event(e, arrive)

    @pl.loop(1, n_all)
    def _(k):
        shuf_copy(k, partner(k)[0]).wait_recv()

    for p in range(n_perm):
        mine = shuf[p * n_subj + subj]
        scol[p] = jnp.transpose(jnp.broadcast_to(mine, (rows, rows)))

    @pl.loop(0, busy)
    def _(turn):
        @pl.loop(0, per_event)
        def _(t):
            move(turn * per_event + t)

        e = BEFORE + turn

        event(e, arrive)

    @pl.loop(early, early + n_mixed)
    def _(e):
        add_dist(e - early)
        event(e, arrive)

    @pl.loop(early + n_mixed, n_events)
    def _(e):
        event(e, arrive)

    @pl.loop(n_mixed, n_z)
    def _(dist):
        add_dist(dist)

    for p in range(n_perm):
        at = p * 2 * rows
        moved = acc[at + rows:at + 2 * rows]
        cross = jnp.sum(moved * (acc[at:at + rows] - kin_diag * moved), axis=0, keepdims=True)
        parts[p, 0:1] = cross

    def fin_copy(k, slot):
        other, device = partner(k)
        return pltpu.make_async_remote_copy(
            src_ref=parts.at[other // n_subj], dst_ref=final.at[slot],
            send_sem=fin_send.at[k], recv_sem=fin_recv.at[slot],
            device_id=device, device_id_type=MESH)

    @pl.loop(1, n_all)
    def _(k):
        fin_copy(k, me).start()

    final[me] = parts[perm]
    own_sends(0, HALVES, lambda copy: copy.wait_send())

    @pl.loop(0, n_events)
    def _(e):
        event(e, drain)

    @pl.loop(1, n_all)
    def _(k):
        shuf_copy(k, me).wait_send()

    @pl.loop(1, n_all)
    def _(k):
        fin_copy(k, partner(k)[0]).wait_recv()

    count = n_subj * rows
    for q in range(n_perm):
        total = jnp.sum(final[q * n_subj:(q + 1) * n_subj], axis=0)
        scale = jnp.sqrt(jnp.float32(count)) * (total[1:2] / count + 1e-05)
        out_ref[:, q * cols:(q + 1) * cols] = total[0:1] / scale

    @pl.loop(1, n_all)
    def _(k):
        fin_copy(k, me).wait_send()


def per_device(n_perm, n_subj, kinship, phenotype, shuffle):
    rows, width = phenotype.shape
    cols = width // n_perm
    n_all = n_perm * n_subj
    DMA = pltpu.SemaphoreType.DMA
    out = pl.pallas_call(
        functools.partial(kernel, n_perm, n_subj),
        out_shape=jax.ShapeDtypeStruct((1, width), jnp.float32),
        in_specs=[pl.BlockSpec(memory_space=pl.ANY)] * 2 + [pl.BlockSpec(memory_space=pltpu.VMEM)],
        out_specs=pl.BlockSpec(memory_space=pltpu.VMEM),
        scratch_shapes=[
            pltpu.VMEM(kinship.shape, jnp.bfloat16),
            DMA((2,)),
            pltpu.SemaphoreType.REGULAR((4,)),
            pltpu.VMEM((n_all, 1, rows), jnp.int32),
            pltpu.VMEM((n_perm, rows, rows), jnp.int32),
            pltpu.VMEM((n_subj, n_perm * 2 * rows, rows), jnp.bfloat16),
            pltpu.VMEM((n_subj, rows, cols), jnp.bfloat16),
            pltpu.VMEM((n_perm * 2 * rows, cols), jnp.float32),
            pltpu.VMEM((n_perm, 2, cols), jnp.float32),
            pltpu.VMEM((n_all, 2, cols), jnp.float32),
            DMA((n_all,)), DMA((n_all,)),
            DMA((3, HALVES)),
            DMA((n_subj, HALVES)), DMA((n_subj, HALVES)), DMA((n_subj, HALVES)),
            DMA((n_all,)), DMA((n_all,)),
        ],
        compiler_params=pltpu.CompilerParams(collective_id=0, has_side_effects=True),
    )(kinship, phenotype, shuffle.reshape(1, rows))
    return out.reshape(width)


def solution(mesh):
    in_specs = (P("subj", None), P("subj", "vert"), P(("perm", "subj")))
    out_specs = P(("perm", "vert"))
    body = functools.partial(per_device, mesh.shape["perm"], mesh.shape["subj"])
    return jax.shard_map(body, mesh=mesh, in_specs=in_specs, out_specs=out_specs, check_vma=False)
```

```python
import functools

import jax
import jax.numpy as jnp
from jax import lax
from jax.experimental import pallas as pl
from jax.experimental.pallas import tpu as pltpu
from jax.sharding import PartitionSpec as P

MESH = pl.DeviceIdType.MESH
CORES = 2
HALVES = 8
BEFORE = 4


def kernel(
    n_perm, n_subj,
    kin_hbm, phe_ref, shf_ref, out_ref,
    kin_ref, load_sem, waves, sq_own, sq_all, sq_send, sq_recv, shuf, scol, moved_kin, gathered, acc, parts, final,
    shuf_send, shuf_recv, own_send, row_send, sib_send, row_recv, fin_send, fin_recv,
):
    perm, subj = lax.axis_index("perm"), lax.axis_index("subj")
    n_all = n_perm * n_subj
    me = perm * n_subj + subj
    z, core = subj // CORES, subj % CORES
    n_z = n_subj // CORES
    sibling = z * CORES + (1 - core)
    rows = kin_ref.shape[0]
    cols = gathered.shape[2]
    piece = rows // HALVES
    first_col = pl.multiple_of(perm * cols, cols)
    n_events = HALVES * (n_z - 1)

    def partner(k):
        other = lax.rem(me + k, n_all)
        return other, {"perm": other // n_subj, "subj": lax.rem(other, n_subj)}

    loads = (
        pltpu.make_async_copy(
            phe_ref.at[:, pl.ds(first_col, cols)], gathered.at[subj], load_sem.at[0]),
        pltpu.make_async_copy(kin_hbm, kin_ref, load_sem.at[1]),
    )
    for load in loads:
        load.start()
    barrier = pltpu.get_barrier_semaphore()

    has_left, has_right = z > 0, z < n_z - 1

    def signal(sem, **device):
        pl.semaphore_signal(sem, inc=1, device_id=device, device_id_type=MESH)

    def signal_perms(sem):
        for k in range(1, n_perm):
            signal(sem, perm=lax.rem(perm + k, n_perm))

    @pl.when(has_left)
    def _():
        signal(barrier, subj=subj - CORES)

    @pl.when(has_right)
    def _():
        signal(barrier, subj=subj + CORES)

    signal(barrier, subj=sibling)
    signal_perms(barrier)
    pl.semaphore_wait(
        barrier, n_perm + has_left.astype(jnp.int32) + has_right.astype(jnp.int32))

    def wave_right():
        @pl.when(has_left)
        def _():
            pl.semaphore_wait(waves.at[0], 1)

        @pl.when(has_right)
        def _():
            signal(waves.at[0], subj=subj + CORES)

    def wave_left():
        @pl.when(has_right)
        def _():
            pl.semaphore_wait(waves.at[1], 1)

        @pl.when(has_left)
        def _():
            signal(waves.at[1], subj=subj - CORES)

    def all_ready():
        @pl.when(z < n_z // 2)
        def _():
            wave_right()
            wave_left()

        @pl.when(z >= n_z // 2)
        def _():
            wave_left()
            wave_right()

        signal(waves.at[2], subj=sibling)
        pl.semaphore_wait(waves.at[2], 1)
        signal_perms(waves.at[3])
        pl.semaphore_wait(waves.at[3], n_perm - 1)

    def half(h):
        return pl.ds(pl.multiple_of(h * piece, piece), piece)

    def own_copy(h, way, target):
        return pltpu.make_async_remote_copy(
            src_ref=phe_ref.at[half(h), pl.ds(first_col, cols)],
            dst_ref=gathered.at[subj, half(h)],
            send_sem=own_send.at[way, h], recv_sem=row_recv.at[subj, h],
            device_id={"subj": target}, device_id_type=MESH)

    def pass_copy(slot, h, sems, target):
        return pltpu.make_async_remote_copy(
            src_ref=gathered.at[slot, half(h)], dst_ref=gathered.at[slot, half(h)],
            send_sem=sems.at[slot, h], recv_sem=row_recv.at[slot, h],
            device_id={"subj": target}, device_id_type=MESH)

    def shuf_copy(k, slot):
        return pltpu.make_async_remote_copy(
            src_ref=shf_ref, dst_ref=shuf.at[slot],
            send_sem=shuf_send.at[k], recv_sem=shuf_recv.at[slot],
            device_id=partner(k)[1], device_id_type=MESH)

    def own_sends(first, last, act):
        for h in range(first, last):
            @pl.when(z > 0)
            def _():
                act(own_copy(h, 0, subj - CORES))

            @pl.when(z < n_z - 1)
            def _():
                act(own_copy(h, 1, subj + CORES))

            act(own_copy(h, 2, sibling))

    own_sends(0, HALVES - 1, lambda copy: copy.start())
    all_ready()

    @pl.loop(1, n_all)
    def _(k):
        shuf_copy(k, me).start()

    own_sends(HALVES - 1, HALVES, lambda copy: copy.start())
    shuf[me] = shf_ref[...]
    for load in loads:
        load.wait()
    own32 = gathered[subj].astype(jnp.float32)
    squares = jnp.sum(own32 * own32, axis=0, keepdims=True)
    sq_own[...] = squares
    sq_all[me] = squares

    def sq_copy(k, slot):
        return pltpu.make_async_remote_copy(
            src_ref=sq_own, dst_ref=sq_all.at[slot],
            send_sem=sq_send.at[k], recv_sem=sq_recv.at[slot],
            device_id=partner(k)[1], device_id_type=MESH)

    @pl.loop(1, n_all)
    def _(k):
        sq_copy(k, me).start()

    own_cols = pl.ds(pl.multiple_of(subj * rows, rows), rows)
    down = lax.broadcasted_iota(jnp.int32, (rows, rows), 0)
    across = lax.broadcasted_iota(jnp.int32, (rows, rows), 1)
    kin_diag = jnp.sum(
        jnp.where(down == across, kin_ref[:, own_cols].astype(jnp.float32), 0.0),
        axis=1, keepdims=True)

    def move(task):
        p, block = task // n_subj, lax.rem(task, n_subj)
        base = down + block * rows
        picks = jnp.concatenate(
            [(base == shuf[p * n_subj + j]).astype(jnp.bfloat16) for j in range(n_subj)],
            axis=1)
        kin = lax.dot_general(
            kin_ref[...], picks, (((1,), (1,)), ((), ())),
            preferred_element_type=jnp.float32)
        at = pl.multiple_of(p * 2 * rows, 2 * rows)
        moved_kin[block, pl.ds(at, rows)] = kin.astype(jnp.bfloat16)
        picker = (scol[p] == across + block * rows).astype(jnp.bfloat16)
        moved_kin[block, pl.ds(at + rows, rows)] = picker

    def event(e, act):
        dist, h = e // HALVES + 1, lax.rem(e, HALVES)

        @pl.when(z + dist < n_z)
        def _():
            act(subj + CORES * dist, h, z > 0, subj - CORES)

        @pl.when(z - dist >= 0)
        def _():
            act(subj - CORES * dist, h, z < n_z - 1, subj + CORES)

    def arrive(slot, h, onward, target):
        pass_copy(slot, h, row_send, sibling).wait_recv()

        @pl.when(onward)
        def _():
            pass_copy(slot, h, row_send, target).start()

        pass_copy(slot, h, sib_send, sibling).start()

    def drain(slot, h, onward, target):
        @pl.when(onward)
        def _():
            pass_copy(slot, h, row_send, target).wait_send()

        pass_copy(slot, h, sib_send, sibling).wait_send()

    def add(slot):
        acc[...] += jnp.dot(
            moved_kin[slot], gathered[slot], preferred_element_type=jnp.float32)

    def await_sibling(slot):
        for h in range(HALVES):
            pass_copy(slot, h, row_send, sibling).wait_recv()

    def add_dist(dist):
        def pair(slot, other):
            add(slot)
            await_sibling(other)
            add(other)

        flip = sibling - subj

        @pl.when(z + dist < n_z)
        def _():
            pair(subj + CORES * dist, subj + CORES * dist + flip)

        @pl.when(jnp.logical_and(z - dist >= 0, dist > 0))
        def _():
            pair(subj - CORES * dist, subj - CORES * dist + flip)

    n_tasks = n_perm * n_subj
    busy = HALVES * n_z // 2
    per_event = n_tasks // busy
    early = min(BEFORE + busy, n_events)
    acc[...] = jnp.zeros_like(acc)
    for e in range(BEFORE):
        event(e, arrive)

    @pl.loop(1, n_all)
    def _(k):
        shuf_copy(k, partner(k)[0]).wait_recv()

    for p in range(n_perm):
        mine = shuf[p * n_subj + subj]
        scol[p] = jnp.transpose(jnp.broadcast_to(mine, (rows, rows)))

    @pl.loop(0, busy)
    def _(turn):
        @pl.loop(0, per_event)
        def _(t):
            move(turn * per_event + t)

        e = BEFORE + turn

        event(e, arrive)

    late = n_events - early

    @pl.loop(0, late)
    def _(turn):
        @pl.loop(turn * (n_z - 1) // late, (turn + 1) * (n_z - 1) // late)
        def _(dist):
            add_dist(dist)

        event(early + turn, arrive)

    add_dist(n_z - 1)

    for p in range(n_perm):
        at = p * 2 * rows
        moved = acc[at + rows:at + 2 * rows]
        cross = jnp.sum(moved * (acc[at:at + rows] - kin_diag * moved), axis=0, keepdims=True)
        parts[p] = cross

    def fin_copy(k, slot):
        other, device = partner(k)
        return pltpu.make_async_remote_copy(
            src_ref=parts.at[other // n_subj], dst_ref=final.at[slot],
            send_sem=fin_send.at[k], recv_sem=fin_recv.at[slot],
            device_id=device, device_id_type=MESH)

    @pl.loop(1, n_all)
    def _(k):
        fin_copy(k, me).start()

    final[me] = parts[perm]
    own_sends(0, HALVES, lambda copy: copy.wait_send())

    @pl.loop(0, n_events)
    def _(e):
        event(e, drain)

    @pl.loop(1, n_all)
    def _(k):
        shuf_copy(k, me).wait_send()
        sq_copy(k, me).wait_send()
        sq_copy(k, partner(k)[0]).wait_recv()

    count = n_subj * rows
    scales = [
        jnp.sqrt(jnp.float32(count))
        * (jnp.sum(sq_all[q * n_subj:(q + 1) * n_subj], axis=0) / count + 1e-05)
        for q in range(n_perm)]

    @pl.loop(1, n_all)
    def _(k):
        fin_copy(k, partner(k)[0]).wait_recv()

    for q in range(n_perm):
        total = jnp.sum(final[q * n_subj:(q + 1) * n_subj], axis=0)
        out_ref[:, q * cols:(q + 1) * cols] = total / scales[q]

    @pl.loop(1, n_all)
    def _(k):
        fin_copy(k, me).wait_send()


def per_device(n_perm, n_subj, kinship, phenotype, shuffle):
    rows, width = phenotype.shape
    cols = width // n_perm
    n_all = n_perm * n_subj
    DMA = pltpu.SemaphoreType.DMA
    out = pl.pallas_call(
        functools.partial(kernel, n_perm, n_subj),
        out_shape=jax.ShapeDtypeStruct((1, width), jnp.float32),
        in_specs=[pl.BlockSpec(memory_space=pl.ANY)] * 2 + [pl.BlockSpec(memory_space=pltpu.VMEM)],
        out_specs=pl.BlockSpec(memory_space=pltpu.VMEM),
        scratch_shapes=[
            pltpu.VMEM(kinship.shape, jnp.bfloat16),
            DMA((2,)),
            pltpu.SemaphoreType.REGULAR((4,)),
            pltpu.VMEM((1, cols), jnp.float32),
            pltpu.VMEM((n_all, 1, cols), jnp.float32),
            DMA((n_all,)), DMA((n_all,)),
            pltpu.VMEM((n_all, 1, rows), jnp.int32),
            pltpu.VMEM((n_perm, rows, rows), jnp.int32),
            pltpu.VMEM((n_subj, n_perm * 2 * rows, rows), jnp.bfloat16),
            pltpu.VMEM((n_subj, rows, cols), jnp.bfloat16),
            pltpu.VMEM((n_perm * 2 * rows, cols), jnp.float32),
            pltpu.VMEM((n_perm, 1, cols), jnp.float32),
            pltpu.VMEM((n_all, 1, cols), jnp.float32),
            DMA((n_all,)), DMA((n_all,)),
            DMA((3, HALVES)),
            DMA((n_subj, HALVES)), DMA((n_subj, HALVES)), DMA((n_subj, HALVES)),
            DMA((n_all,)), DMA((n_all,)),
        ],
        compiler_params=pltpu.CompilerParams(collective_id=0, has_side_effects=True),
    )(kinship, phenotype, shuffle.reshape(1, rows))
    return out.reshape(width)


def solution(mesh):
    in_specs = (P("subj", None), P("subj", "vert"), P(("perm", "subj")))
    out_specs = P(("perm", "vert"))
    body = functools.partial(per_device, mesh.shape["perm"], mesh.shape["subj"])
    return jax.shard_map(body, mesh=mesh, in_specs=in_specs, out_specs=out_specs, check_vma=False)
```

```python
import functools

import jax
import jax.numpy as jnp
from jax import lax
from jax.experimental import pallas as pl
from jax.experimental.pallas import tpu as pltpu
from jax.sharding import PartitionSpec as P

MESH = pl.DeviceIdType.MESH
CORES = 2
HALVES = 4
BEFORE = 2


def kernel(
    n_perm, n_subj,
    kin_hbm, phe_ref, shf_ref, out_ref,
    kin_ref, load_sem, waves, shuf, scol, moved_kin, gathered, acc, parts, final,
    shuf_send, shuf_recv, own_send, row_send, sib_send, row_recv, fin_send, fin_recv,
):
    perm, subj = lax.axis_index("perm"), lax.axis_index("subj")
    n_all = n_perm * n_subj
    me = perm * n_subj + subj
    z, core = subj // CORES, subj % CORES
    n_z = n_subj // CORES
    sibling = z * CORES + (1 - core)
    rows = kin_ref.shape[0]
    cols = gathered.shape[2]
    piece = rows // HALVES
    first_col = pl.multiple_of(perm * cols, cols)
    n_events = HALVES * (n_z - 1)

    def partner(k):
        other = lax.rem(me + k, n_all)
        return other, {"perm": other // n_subj, "subj": lax.rem(other, n_subj)}

    loads = (
        pltpu.make_async_copy(
            phe_ref.at[:, pl.ds(first_col, cols)], gathered.at[subj], load_sem.at[0]),
        pltpu.make_async_copy(kin_hbm, kin_ref, load_sem.at[1]),
    )
    for load in loads:
        load.start()
    barrier = pltpu.get_barrier_semaphore()

    has_left, has_right = z > 0, z < n_z - 1

    def signal(sem, **device):
        pl.semaphore_signal(sem, inc=1, device_id=device, device_id_type=MESH)

    def signal_perms(sem):
        for k in range(1, n_perm):
            signal(sem, perm=lax.rem(perm + k, n_perm))

    @pl.when(has_left)
    def _():
        signal(barrier, subj=subj - CORES)

    @pl.when(has_right)
    def _():
        signal(barrier, subj=subj + CORES)

    signal(barrier, subj=sibling)
    signal_perms(barrier)
    pl.semaphore_wait(
        barrier, n_perm + has_left.astype(jnp.int32) + has_right.astype(jnp.int32))

    def wave_right():
        @pl.when(has_left)
        def _():
            pl.semaphore_wait(waves.at[0], 1)

        @pl.when(has_right)
        def _():
            signal(waves.at[0], subj=subj + CORES)

    def wave_left():
        @pl.when(has_right)
        def _():
            pl.semaphore_wait(waves.at[1], 1)

        @pl.when(has_left)
        def _():
            signal(waves.at[1], subj=subj - CORES)

    def all_ready():
        @pl.when(z < n_z // 2)
        def _():
            wave_right()
            wave_left()

        @pl.when(z >= n_z // 2)
        def _():
            wave_left()
            wave_right()

        signal(waves.at[2], subj=sibling)
        pl.semaphore_wait(waves.at[2], 1)
        signal_perms(waves.at[3])
        pl.semaphore_wait(waves.at[3], n_perm - 1)

    def half(h):
        return pl.ds(pl.multiple_of(h * piece, piece), piece)

    def own_copy(h, way, target):
        return pltpu.make_async_remote_copy(
            src_ref=phe_ref.at[half(h), pl.ds(first_col, cols)],
            dst_ref=gathered.at[subj, half(h)],
            send_sem=own_send.at[way, h], recv_sem=row_recv.at[subj, h],
            device_id={"subj": target}, device_id_type=MESH)

    def pass_copy(slot, h, sems, target):
        return pltpu.make_async_remote_copy(
            src_ref=gathered.at[slot, half(h)], dst_ref=gathered.at[slot, half(h)],
            send_sem=sems.at[slot, h], recv_sem=row_recv.at[slot, h],
            device_id={"subj": target}, device_id_type=MESH)

    def shuf_copy(k, slot):
        return pltpu.make_async_remote_copy(
            src_ref=shf_ref, dst_ref=shuf.at[slot],
            send_sem=shuf_send.at[k], recv_sem=shuf_recv.at[slot],
            device_id=partner(k)[1], device_id_type=MESH)

    def own_sends(first, last, act):
        for h in range(first, last):
            @pl.when(z > 0)
            def _():
                act(own_copy(h, 0, subj - CORES))

            @pl.when(z < n_z - 1)
            def _():
                act(own_copy(h, 1, subj + CORES))

            act(own_copy(h, 2, sibling))

    own_sends(0, HALVES - 1, lambda copy: copy.start())
    all_ready()

    @pl.loop(1, n_all)
    def _(k):
        shuf_copy(k, me).start()

    own_sends(HALVES - 1, HALVES, lambda copy: copy.start())
    shuf[me] = shf_ref[...]
    for load in loads:
        load.wait()
    own32 = gathered[subj].astype(jnp.float32)
    squares = jnp.sum(own32 * own32, axis=0, keepdims=True)
    for p in range(n_perm):
        parts[p, 1:2] = squares
    own_cols = pl.ds(pl.multiple_of(subj * rows, rows), rows)
    down = lax.broadcasted_iota(jnp.int32, (rows, rows), 0)
    across = lax.broadcasted_iota(jnp.int32, (rows, rows), 1)
    kin_diag = jnp.sum(
        jnp.where(down == across, kin_ref[:, own_cols].astype(jnp.float32), 0.0),
        axis=1, keepdims=True)

    def move(task):
        p, block = task // n_subj, lax.rem(task, n_subj)
        base = down + block * rows
        picks = jnp.concatenate(
            [(base == shuf[p * n_subj + j]).astype(jnp.bfloat16) for j in range(n_subj)],
            axis=1)
        kin = lax.dot_general(
            kin_ref[...], picks, (((1,), (1,)), ((), ())),
            preferred_element_type=jnp.float32)
        at = pl.multiple_of(p * 2 * rows, 2 * rows)
        moved_kin[block, pl.ds(at, rows)] = kin.astype(jnp.bfloat16)
        picker = (scol[p] == across + block * rows).astype(jnp.bfloat16)
        moved_kin[block, pl.ds(at + rows, rows)] = picker

    def event(e, act):
        dist, h = e // HALVES + 1, lax.rem(e, HALVES)

        @pl.when(z + dist < n_z)
        def _():
            act(subj + CORES * dist, h, z > 0, subj - CORES)

        @pl.when(z - dist >= 0)
        def _():
            act(subj - CORES * dist, h, z < n_z - 1, subj + CORES)

    def arrive(slot, h, onward, target):
        pass_copy(slot, h, row_send, sibling).wait_recv()

        @pl.when(onward)
        def _():
            pass_copy(slot, h, row_send, target).start()

        pass_copy(slot, h, sib_send, sibling).start()

    def drain(slot, h, onward, target):
        @pl.when(onward)
        def _():
            pass_copy(slot, h, row_send, target).wait_send()

        pass_copy(slot, h, sib_send, sibling).wait_send()

    def add(slot):
        acc[...] += jnp.dot(
            moved_kin[slot], gathered[slot], preferred_element_type=jnp.float32)

    def await_sibling(slot):
        for h in range(HALVES):
            pass_copy(slot, h, row_send, sibling).wait_recv()

    def add_dist(dist):
        def pair(slot, other):
            add(slot)
            await_sibling(other)
            add(other)

        flip = sibling - subj

        @pl.when(z + dist < n_z)
        def _():
            pair(subj + CORES * dist, subj + CORES * dist + flip)

        @pl.when(jnp.logical_and(z - dist >= 0, dist > 0))
        def _():
            pair(subj - CORES * dist, subj - CORES * dist + flip)

    n_tasks = n_perm * n_subj
    busy = HALVES * n_z // 2
    per_event = n_tasks // busy
    early = min(BEFORE + busy, n_events)
    acc[...] = jnp.zeros_like(acc)
    for e in range(BEFORE):
        event(e, arrive)

    @pl.loop(1, n_all)
    def _(k):
        shuf_copy(k, partner(k)[0]).wait_recv()

    for p in range(n_perm):
        mine = shuf[p * n_subj + subj]
        scol[p] = jnp.transpose(jnp.broadcast_to(mine, (rows, rows)))

    @pl.loop(0, busy)
    def _(turn):
        @pl.loop(0, per_event)
        def _(t):
            move(turn * per_event + t)

        e = BEFORE + turn

        event(e, arrive)

    late = n_events - early

    @pl.loop(0, late)
    def _(turn):
        @pl.loop(turn * (n_z - 1) // late, (turn + 1) * (n_z - 1) // late)
        def _(dist):
            add_dist(dist)

        event(early + turn, arrive)

    add_dist(n_z - 1)

    for p in range(n_perm):
        at = p * 2 * rows
        moved = acc[at + rows:at + 2 * rows]
        cross = jnp.sum(moved * (acc[at:at + rows] - kin_diag * moved), axis=0, keepdims=True)
        parts[p, 0:1] = cross

    per_z = n_all // n_z
    far_low = (z >= n_z // 2).astype(jnp.int32)

    def fin_copy(k, slot):
        turn, rest = k // per_z, lax.rem(k, per_z)
        to_z = far_low * turn + (1 - far_low) * (n_z - 1 - turn)
        to_perm, to_subj = rest // CORES, to_z * CORES + lax.rem(rest, CORES)
        copy = pltpu.make_async_remote_copy(
            src_ref=parts.at[to_perm], dst_ref=final.at[slot],
            send_sem=fin_send.at[k], recv_sem=fin_recv.at[slot],
            device_id={"perm": to_perm, "subj": to_subj}, device_id_type=MESH)
        return copy, to_perm * n_subj + to_subj != me

    @pl.loop(0, n_all)
    def _(k):
        copy, other = fin_copy(k, me)
        pl.when(other)(copy.start)

    final[me] = parts[perm]
    own_sends(0, HALVES, lambda copy: copy.wait_send())

    @pl.loop(0, n_events)
    def _(e):
        event(e, drain)

    @pl.loop(1, n_all)
    def _(k):
        shuf_copy(k, me).wait_send()

    @pl.loop(1, n_all)
    def _(k):
        fin_copy(0, partner(k)[0])[0].wait_recv()

    count = n_subj * rows
    for q in range(n_perm):
        total = jnp.sum(final[q * n_subj:(q + 1) * n_subj], axis=0)
        scale = jnp.sqrt(jnp.float32(count)) * (total[1:2] / count + 1e-05)
        out_ref[:, q * cols:(q + 1) * cols] = total[0:1] / scale

    @pl.loop(0, n_all)
    def _(k):
        copy, other = fin_copy(k, me)
        pl.when(other)(copy.wait_send)


def per_device(n_perm, n_subj, kinship, phenotype, shuffle):
    rows, width = phenotype.shape
    cols = width // n_perm
    n_all = n_perm * n_subj
    DMA = pltpu.SemaphoreType.DMA
    out = pl.pallas_call(
        functools.partial(kernel, n_perm, n_subj),
        out_shape=jax.ShapeDtypeStruct((1, width), jnp.float32),
        in_specs=[pl.BlockSpec(memory_space=pl.ANY)] * 2 + [pl.BlockSpec(memory_space=pltpu.VMEM)],
        out_specs=pl.BlockSpec(memory_space=pltpu.VMEM),
        scratch_shapes=[
            pltpu.VMEM(kinship.shape, jnp.bfloat16),
            DMA((2,)),
            pltpu.SemaphoreType.REGULAR((4,)),
            pltpu.VMEM((n_all, 1, rows), jnp.int32),
            pltpu.VMEM((n_perm, rows, rows), jnp.int32),
            pltpu.VMEM((n_subj, n_perm * 2 * rows, rows), jnp.bfloat16),
            pltpu.VMEM((n_subj, rows, cols), jnp.bfloat16),
            pltpu.VMEM((n_perm * 2 * rows, cols), jnp.float32),
            pltpu.VMEM((n_perm, 2, cols), jnp.float32),
            pltpu.VMEM((n_all, 2, cols), jnp.float32),
            DMA((n_all,)), DMA((n_all,)),
            DMA((3, HALVES)),
            DMA((n_subj, HALVES)), DMA((n_subj, HALVES)), DMA((n_subj, HALVES)),
            DMA((n_all,)), DMA((n_all,)),
        ],
        compiler_params=pltpu.CompilerParams(collective_id=0, has_side_effects=True),
    )(kinship, phenotype, shuffle.reshape(1, rows))
    return out.reshape(width)


def solution(mesh):
    in_specs = (P("subj", None), P("subj", "vert"), P(("perm", "subj")))
    out_specs = P(("perm", "vert"))
    body = functools.partial(per_device, mesh.shape["perm"], mesh.shape["subj"])
    return jax.shard_map(body, mesh=mesh, in_specs=in_specs, out_specs=out_specs, check_vma=False)
```

```python
import functools

import jax
import jax.numpy as jnp
from jax import lax
from jax.experimental import pallas as pl
from jax.experimental.pallas import tpu as pltpu
from jax.sharding import PartitionSpec as P

MESH = pl.DeviceIdType.MESH
CORES = 2
HALVES = 4
BEFORE = 2


def kernel(
    n_perm, n_subj,
    kin_hbm, phe_ref, shf_ref, out_ref,
    kin_ref, load_sem, waves, shuf, scol, moved_kin, gathered, acc, parts, final,
    shuf_send, shuf_recv, own_send, row_send, sib_send, row_recv, fin_send, fin_recv,
):
    perm, subj = lax.axis_index("perm"), lax.axis_index("subj")
    n_all = n_perm * n_subj
    me = perm * n_subj + subj
    z, core = subj // CORES, subj % CORES
    n_z = n_subj // CORES
    sibling = z * CORES + (1 - core)
    rows = kin_ref.shape[0]
    cols = gathered.shape[2]
    piece = rows // HALVES
    first_col = pl.multiple_of(perm * cols, cols)
    n_events = HALVES * (n_z - 1)

    def partner(k):
        other = lax.rem(me + k, n_all)
        return other, {"perm": other // n_subj, "subj": lax.rem(other, n_subj)}

    loads = (
        pltpu.make_async_copy(
            phe_ref.at[:, pl.ds(first_col, cols)], gathered.at[subj], load_sem.at[0]),
        pltpu.make_async_copy(kin_hbm, kin_ref, load_sem.at[1]),
    )
    for load in loads:
        load.start()
    barrier = pltpu.get_barrier_semaphore()

    has_left, has_right = z > 0, z < n_z - 1

    def signal(sem, **device):
        pl.semaphore_signal(sem, inc=1, device_id=device, device_id_type=MESH)

    def signal_perms(sem):
        for k in range(1, n_perm):
            signal(sem, perm=lax.rem(perm + k, n_perm))

    @pl.when(has_left)
    def _():
        signal(barrier, subj=subj - CORES)

    @pl.when(has_right)
    def _():
        signal(barrier, subj=subj + CORES)

    signal(barrier, subj=sibling)
    signal_perms(barrier)
    pl.semaphore_wait(
        barrier, n_perm + has_left.astype(jnp.int32) + has_right.astype(jnp.int32))

    def wave_right():
        @pl.when(has_left)
        def _():
            pl.semaphore_wait(waves.at[0], 1)

        @pl.when(has_right)
        def _():
            signal(waves.at[0], subj=subj + CORES)

    def wave_left():
        @pl.when(has_right)
        def _():
            pl.semaphore_wait(waves.at[1], 1)

        @pl.when(has_left)
        def _():
            signal(waves.at[1], subj=subj - CORES)

    def all_ready():
        @pl.when(z < n_z // 2)
        def _():
            wave_right()
            wave_left()

        @pl.when(z >= n_z // 2)
        def _():
            wave_left()
            wave_right()

        signal(waves.at[2], subj=sibling)
        pl.semaphore_wait(waves.at[2], 1)
        signal_perms(waves.at[3])
        pl.semaphore_wait(waves.at[3], n_perm - 1)

    def half(h):
        return pl.ds(pl.multiple_of(h * piece, piece), piece)

    def own_copy(h, way, target):
        return pltpu.make_async_remote_copy(
            src_ref=phe_ref.at[half(h), pl.ds(first_col, cols)],
            dst_ref=gathered.at[subj, half(h)],
            send_sem=own_send.at[way, h], recv_sem=row_recv.at[subj, h],
            device_id={"subj": target}, device_id_type=MESH)

    def pass_copy(slot, h, sems, target):
        return pltpu.make_async_remote_copy(
            src_ref=gathered.at[slot, half(h)], dst_ref=gathered.at[slot, half(h)],
            send_sem=sems.at[slot, h], recv_sem=row_recv.at[slot, h],
            device_id={"subj": target}, device_id_type=MESH)

    def shuf_copy(k, slot):
        return pltpu.make_async_remote_copy(
            src_ref=shf_ref, dst_ref=shuf.at[slot],
            send_sem=shuf_send.at[k], recv_sem=shuf_recv.at[slot],
            device_id=partner(k)[1], device_id_type=MESH)

    def own_sends(first, last, act):
        for h in range(first, last):
            @pl.when(z > 0)
            def _():
                act(own_copy(h, 0, subj - CORES))

            @pl.when(z < n_z - 1)
            def _():
                act(own_copy(h, 1, subj + CORES))

            act(own_copy(h, 2, sibling))

    own_sends(0, HALVES - 1, lambda copy: copy.start())
    all_ready()

    @pl.loop(1, n_all)
    def _(k):
        shuf_copy(k, me).start()

    own_sends(HALVES - 1, HALVES, lambda copy: copy.start())
    shuf[me] = shf_ref[...]
    for load in loads:
        load.wait()
    own32 = gathered[subj].astype(jnp.float32)
    squares = jnp.sum(own32 * own32, axis=0, keepdims=True)
    for p in range(n_perm):
        parts[p, 1:2] = squares
    own_cols = pl.ds(pl.multiple_of(subj * rows, rows), rows)
    down = lax.broadcasted_iota(jnp.int32, (rows, rows), 0)
    across = lax.broadcasted_iota(jnp.int32, (rows, rows), 1)
    kin_diag = jnp.sum(
        jnp.where(down == across, kin_ref[:, own_cols].astype(jnp.float32), 0.0),
        axis=1, keepdims=True)

    def move(task):
        p, block = task // n_subj, lax.rem(task, n_subj)
        base = down + block * rows
        picks = jnp.concatenate(
            [(base == shuf[p * n_subj + j]).astype(jnp.bfloat16) for j in range(n_subj)],
            axis=1)
        kin = lax.dot_general(
            kin_ref[...], picks, (((1,), (1,)), ((), ())),
            preferred_element_type=jnp.float32)
        at = pl.multiple_of(p * 2 * rows, 2 * rows)
        moved_kin[block, pl.ds(at, rows)] = kin.astype(jnp.bfloat16)
        picker = (scol[p] == across + block * rows).astype(jnp.bfloat16)
        moved_kin[block, pl.ds(at + rows, rows)] = picker

    def event(e, act):
        dist, h = e // HALVES + 1, lax.rem(e, HALVES)

        @pl.when(z + dist < n_z)
        def _():
            act(subj + CORES * dist, h, z > 0, subj - CORES)

        @pl.when(z - dist >= 0)
        def _():
            act(subj - CORES * dist, h, z < n_z - 1, subj + CORES)

    def arrive(slot, h, onward, target):
        pass_copy(slot, h, row_send, sibling).wait_recv()

        @pl.when(onward)
        def _():
            pass_copy(slot, h, row_send, target).start()

        pass_copy(slot, h, sib_send, sibling).start()

    def drain(slot, h, onward, target):
        @pl.when(onward)
        def _():
            pass_copy(slot, h, row_send, target).wait_send()

        pass_copy(slot, h, sib_send, sibling).wait_send()

    def add(slot):
        acc[...] += jnp.dot(
            moved_kin[slot], gathered[slot], preferred_element_type=jnp.float32)

    def await_sibling(slot):
        for h in range(HALVES):
            pass_copy(slot, h, row_send, sibling).wait_recv()

    def add_dist(dist):
        def pair(slot, other):
            add(slot)
            await_sibling(other)
            add(other)

        flip = sibling - subj

        @pl.when(z + dist < n_z)
        def _():
            pair(subj + CORES * dist, subj + CORES * dist + flip)

        @pl.when(jnp.logical_and(z - dist >= 0, dist > 0))
        def _():
            pair(subj - CORES * dist, subj - CORES * dist + flip)

    n_tasks = n_perm * n_subj
    busy = HALVES * n_z // 2
    per_event = n_tasks // busy
    early = min(BEFORE + busy, n_events)
    acc[...] = jnp.zeros_like(acc)
    for e in range(BEFORE):
        event(e, arrive)

    @pl.loop(1, n_all)
    def _(k):
        shuf_copy(k, partner(k)[0]).wait_recv()

    for p in range(n_perm):
        mine = shuf[p * n_subj + subj]
        scol[p] = jnp.transpose(jnp.broadcast_to(mine, (rows, rows)))

    @pl.loop(0, busy)
    def _(turn):
        @pl.loop(0, per_event)
        def _(t):
            move(turn * per_event + t)

        e = BEFORE + turn

        event(e, arrive)

    late = n_events - early

    @pl.loop(0, late)
    def _(turn):
        @pl.loop(turn * (n_z - 1) // late, (turn + 1) * (n_z - 1) // late)
        def _(dist):
            add_dist(dist)

        event(early + turn, arrive)

    add_dist(n_z - 1)

    for p in range(n_perm):
        at = p * 2 * rows
        moved = acc[at + rows:at + 2 * rows]
        cross = jnp.sum(moved * (acc[at:at + rows] - kin_diag * moved), axis=0, keepdims=True)
        parts[p, 0:1] = cross

    per_z = n_all // n_z
    far_low = (z >= n_z // 2).astype(jnp.int32)

    def fin_copy(k, slot):
        turn, rest = k // per_z, lax.rem(k, per_z)
        to_z = far_low * turn + (1 - far_low) * (n_z - 1 - turn)
        to_perm, to_subj = rest // CORES, to_z * CORES + lax.rem(rest, CORES)
        copy = pltpu.make_async_remote_copy(
            src_ref=parts.at[to_perm], dst_ref=final.at[slot],
            send_sem=fin_send.at[k], recv_sem=fin_recv.at[slot],
            device_id={"perm": to_perm, "subj": to_subj}, device_id_type=MESH)
        return copy, to_perm * n_subj + to_subj != me

    @pl.loop(0, n_all)
    def _(k):
        copy, other = fin_copy(k, me)
        pl.when(other)(copy.start)

    final[me] = parts[perm]
    own_sends(0, HALVES, lambda copy: copy.wait_send())

    @pl.loop(0, n_events)
    def _(e):
        event(e, drain)

    @pl.loop(1, n_all)
    def _(k):
        shuf_copy(k, me).wait_send()

    @pl.loop(1, n_all)
    def _(k):
        fin_copy(0, partner(k)[0])[0].wait_recv()

    for q in range(n_perm):
        total = jnp.sum(final[q * n_subj:(q + 1) * n_subj], axis=0)
        out_ref[:, q * cols:(q + 1) * cols] = total

    @pl.loop(0, n_all)
    def _(k):
        copy, other = fin_copy(k, me)
        pl.when(other)(copy.wait_send)


def per_device(n_perm, n_subj, kinship, phenotype, shuffle):
    rows, width = phenotype.shape
    cols = width // n_perm
    n_all = n_perm * n_subj
    DMA = pltpu.SemaphoreType.DMA
    out = pl.pallas_call(
        functools.partial(kernel, n_perm, n_subj),
        out_shape=jax.ShapeDtypeStruct((2, width), jnp.float32),
        in_specs=[pl.BlockSpec(memory_space=pl.ANY)] * 2 + [pl.BlockSpec(memory_space=pltpu.VMEM)],
        out_specs=pl.BlockSpec(memory_space=pltpu.VMEM),
        scratch_shapes=[
            pltpu.VMEM(kinship.shape, jnp.bfloat16),
            DMA((2,)),
            pltpu.SemaphoreType.REGULAR((4,)),
            pltpu.VMEM((n_all, 1, rows), jnp.int32),
            pltpu.VMEM((n_perm, rows, rows), jnp.int32),
            pltpu.VMEM((n_subj, n_perm * 2 * rows, rows), jnp.bfloat16),
            pltpu.VMEM((n_subj, rows, cols), jnp.bfloat16),
            pltpu.VMEM((n_perm * 2 * rows, cols), jnp.float32),
            pltpu.VMEM((n_perm, 2, cols), jnp.float32),
            pltpu.VMEM((n_all, 2, cols), jnp.float32),
            DMA((n_all,)), DMA((n_all,)),
            DMA((3, HALVES)),
            DMA((n_subj, HALVES)), DMA((n_subj, HALVES)), DMA((n_subj, HALVES)),
            DMA((n_all,)), DMA((n_all,)),
        ],
        compiler_params=pltpu.CompilerParams(collective_id=0, has_side_effects=True),
    )(kinship, phenotype, shuffle.reshape(1, rows))
    count = n_subj * rows
    return out[0] / (jnp.sqrt(jnp.float32(count)) * (out[1] / count + 1e-05))


def solution(mesh):
    in_specs = (P("subj", None), P("subj", "vert"), P(("perm", "subj")))
    out_specs = P(("perm", "vert"))
    body = functools.partial(per_device, mesh.shape["perm"], mesh.shape["subj"])
    return jax.shard_map(body, mesh=mesh, in_specs=in_specs, out_specs=out_specs, check_vma=False)
```
